32 devices in a mesh: row: 8 (over z, x), col: 4 (over y, core).
Axes of the slice: x: 2, y: 2, z: 4, core: 2. Of those that a mesh axis runs over, the one named last changes fastest.
Arguments:
- block_input: float32 [4096, 1024], P(('row', 'col')), as said below
- segment_ids: int32 [8, 512], P('row'), may hold values from 0 to 2, never falling along the last dimension, each value on 1 to 384 neighbouring positions
- expert_routes: int32 [4096, 8], P(('row', 'col')), may hold values from 0 to 31, all different within a row; in each aligned block of 128 rows (0 to 127, 128 to 255, ...) at most 36 rows name the same one
- route_weights: float32 [4096, 8], P(('row', 'col')), may hold values from 0.05 to 0.5
- attn_gain: float32 [1024], replicated, may hold values from 0.5 to 1.5
- mlp_gain: float32 [1024], replicated, may hold values from 0.5 to 1.5
- joined_projection_weight: bfloat16 [1024, 2048], P('row', 'col')
- output_weight: bfloat16 [1024, 1024], P('row', 'col'), may hold values from -1 to 1
- w_gate: bfloat16 [32, 1024, 512], P('row', 'col'), may hold values from -0.1875 to 0.1875
- w_up: bfloat16 [32, 1024, 512], P('row', 'col'), may hold values from -0.1875 to 0.1875
- w_down: bfloat16 [32, 512, 1024], P('row', 'col'), may hold values from -0.5 to 0.5
- out_grad: float32 [4096, 1024], P(('row', 'col')), as said below
Outputs:
- block_output: float32 [4096, 1024], P(('row', 'col'))
- input_grad: float32 [4096, 1024], P(('row', 'col'))
- attn_gain_grad: float32 [1024], replicated
- mlp_gain_grad: float32 [1024], replicated
- w_qkv_grad: float32 [1024, 2048], P('row', 'col')
- w_out_grad: float32 [1024, 1024], P('row', 'col')
- w_gate_grad: float32 [32, 1024, 512], P('row', 'col')
- w_up_grad: float32 [32, 1024, 512], P('row', 'col')
- w_down_grad: float32 [32, 512, 1024], P('row', 'col')
The draws below stay inside these ranges and needn't reach their ends.
Inputs may be any that keep to these rules, and one draw needn't show every extreme that they name: `segment_ids`: each packed row of 512 positions holds whole documents: its ids never fall, each document has 1 to 384 positions, one exactly 384. `expert_routes`: the 8 experts of a token differ. In each aligned block of 128 tokens (the tokens of one device) no expert is named by more than 36 tokens, a bound that some block reaches. `block_input`: feature scales differ from column to column and token scales from row to row. `out_grad`: rows have differing scales.
All inputs are finite; a program needn't handle non-finite values.
Results may differ from the reference program's by a relative error of at most 0.013.
The reference program's roundings to bfloat16 on the way count: a program that leaves them out, or rounds other values in their place, can miss the bound.
Values may be sent and summed in bfloat16 or wider, within the bound.
A program may use at most 128 MiB of HBM per device.

```python
import math
import jax
import jax.numpy as jnp
import numpy as np
from jax import lax

MODEL_WIDTH = 1024
QUERY_HEADS = 16
KEY_VALUE_HEADS = 8
HEAD_SIZE = 64
FF = 512
E = 32
TOP = 8
PACKED_LENGTH = 512
LONGEST = 384
TD = 128
TOKENS = 4096
PACKED_ROWS = 8
CAP = 36
QKV = 2048
HQD = 1024


def draw_block_input(key, part):
    base_key, column_key, row_key = jax.random.split(jax.random.fold_in(key, 11), 3)
    column_scale = jnp.exp(jax.random.uniform(column_key, (1, MODEL_WIDTH), jnp.float32, math.log(0.3), math.log(3.0)))
    rotary_base = jnp.clip(jax.random.normal(base_key, (TOKENS, MODEL_WIDTH), jnp.float32), -5.0, 5.0)
    row_scale = jnp.exp(jax.random.uniform(row_key, (TOKENS, 1), jnp.float32, math.log(0.5), math.log(2.0)))
    return rotary_base * column_scale * row_scale


def draw_out_grad(key, part):
    base_key = jax.random.fold_in(jax.random.fold_in(key, 23), 0)
    ramp = jnp.exp(math.log(3.0) * jnp.arange(TOKENS, dtype=jnp.float32) / max(TOKENS - 1, 1))[:, None]
    rotary_base = jnp.clip(jax.random.normal(base_key, (TOKENS, MODEL_WIDTH), jnp.float32), -5.0, 5.0)
    return rotary_base * ramp


def draw_joined_projection_weight(key, part):
    spread_rows = MODEL_WIDTH ** (-0.5)
    inner_sort_key = jax.random.fold_in(key, 37)
    weight_arrays = jnp.clip(jax.random.normal(inner_sort_key, (MODEL_WIDTH, KEY_VALUE_HEADS, 4, HEAD_SIZE), jnp.float32), -5.0, 5.0) * spread_rows
    return weight_arrays.reshape(MODEL_WIDTH, (QUERY_HEADS + 2 * KEY_VALUE_HEADS) * HEAD_SIZE).astype(jnp.bfloat16)


def levels(own_key, shape, pieces, least, high):
    level, own = 1.0, jax.random.fold_in(own_key, 6)
    for axis_at, blocks in pieces:
        heights = jnp.exp(jax.random.uniform(jax.random.fold_in(own, axis_at), (blocks,), jnp.float32, least / len(pieces), high / len(pieces)))
        level = level * jnp.repeat(heights, shape[axis_at] // blocks).reshape([-1 if axis == axis_at else 1 for axis in range(len(shape))])
    return level


def split_up(amount, total, limit, lean):
    portions = [(1 << 20) // math.isqrt(standing ** lean) + 1 for standing in range(2, amount + 1)]
    rest, counts = total - limit - (amount - 1), [1] * (amount - 1)
    while rest > 0:
        candidates = [i for i in range(amount - 1) if counts[i] < limit]
        mass, budget = sum([portions[i] for i in candidates]), rest
        for i in candidates:
            more = min(limit - counts[i], max(1, budget * portions[i] // mass), rest)
            counts[i] = counts[i] + more
            rest = rest - more
    return np.array([limit] + counts)


def ragged_sizes(own_key, amount, total, bound, lean):
    if amount == 2:
        one = jax.random.randint(own_key, (), max(1, total - bound), min(bound, total - 1) + 1)
        return jnp.stack([one, total - one])
    tallies = jnp.asarray(split_up(amount, total, bound, lean), jnp.int32)
    pairs = (amount - 1) // 2
    donor, taker = tallies[1:1 + 2 * pairs:2], tallies[2:2 + 2 * pairs:2]
    slack = jnp.minimum(donor - 1, bound - taker)
    passed = jax.random.randint(jax.random.fold_in(own_key, 1), (pairs,), 0, 1 << 20) % (slack + 1)
    tallies = tallies.at[1:1 + 2 * pairs:2].set(donor - passed).at[2:2 + 2 * pairs:2].set(taker + passed)
    return tallies[jax.random.permutation(jax.random.fold_in(own_key, 2), amount)]


def routed_block(own_key, own, number, rows, count, top, most, slope):
    order = jax.random.permutation(own_key, count)
    heavy_load, common = shares(count, rows * top, most, slope, True), shares(count, rows * top, most, slope, False)
    places = jnp.arange(count)

    def named(lengths, rotation):
        used = int((lengths > 0).sum())
        fixed = max(1, used // 4)
        moved = fixed + (places - fixed + rotation * (used - fixed)) % max(1, count - fixed)
        return jnp.zeros((count,), jnp.int32).at[order[jnp.where(places < fixed, places, moved)]].set(jnp.asarray(lengths, jnp.int32))

    lengths = jnp.where(number % 4 == 0, named(heavy_load, number // 4), named(common, number - number // 4 - 1))
    mixed = jax.random.permutation(jax.random.fold_in(own, 3), count)
    giver, taker = mixed[0:count // 2 * 2:2], mixed[1:count // 2 * 2:2]
    room = jnp.minimum(lengths[giver] - 1, most - lengths[taker]) // 2
    room = jnp.where((giver == order[0]) | (taker == order[0]) | (lengths[taker] == 0), 0, jnp.maximum(room, 0))
    moved = jax.random.randint(jax.random.fold_in(own, 4), (count // 2,), 0, 1 << 20) % (room + 1)
    lengths = lengths.at[giver].add(-moved).at[taker].add(moved)
    labels = jnp.searchsorted(jnp.cumsum(lengths), jnp.arange(rows * top), side="right").astype(jnp.int32)
    grid = labels.reshape(top, rows).T
    grid = grid[jax.random.permutation(jax.random.fold_in(own, 1), rows)]
    rotation = jax.random.randint(jax.random.fold_in(own, 2), (rows, 1), 0, top)
    return jnp.take_along_axis(grid, (jnp.arange(top)[None, :] + rotation) % top, axis=1)


def shares(count, total, bound, slope, full):
    portions = [(1 << 20) // math.isqrt(grade ** slope) + 1 for grade in range(1, count + 1)]
    largest = bound if full else min(bound, max(-(-total // count), total * portions[0] // sum(portions)))
    least = 1 if total - largest >= count - 1 else 0
    counts, rest = [largest] + [least] * (count - 1), total - largest - least * (count - 1)
    while rest > 0:
        free = [i for i in range(1, count) if counts[i] < largest] or [i for i in range(1, count) if counts[i] < bound]
        whole, remaining = sum([portions[i] for i in free]), rest
        for i in free:
            more = min(bound - counts[i], max(1, remaining * portions[i] // whole), rest)
            counts[i] = counts[i] + more
            rest = rest - more
    return np.array(counts)


def centred(rng, shape, spread, reach, shards=(), held_as=jnp.bfloat16):
    values = spread * jax.random.normal(rng, shape, jnp.float32)
    if shards:
        values = values * levels(rng, shape, shards, -0.22, 0.18)
    return jnp.clip(values, -reach, reach).astype(held_as)


def setup_inputs(seed: int = 0) -> dict:
    keys = jax.random.split(jax.random.key(seed), 13)
    block_input = draw_block_input(jax.random.fold_in(keys[12], 71), 0)
    segment_ids = jax.vmap(lambda own: jnp.searchsorted(jnp.cumsum(ragged_sizes(own, 3, PACKED_LENGTH, LONGEST, 2)), jnp.arange(PACKED_LENGTH), side="right"))(jax.random.split(keys[1], PACKED_ROWS)).reshape((PACKED_ROWS, PACKED_LENGTH)).astype(jnp.int32)
    expert_routes_keys = jax.random.split(jax.random.fold_in(keys[2], 1), TOKENS // TD)
    expert_routes_turns = jax.random.permutation(jax.random.fold_in(keys[2], 3), TOKENS // TD)
    expert_routes = jax.vmap(lambda own, number: routed_block(jax.random.fold_in(keys[2], 2), own, number, TD, E, TOP, CAP, 1))(expert_routes_keys, expert_routes_turns).reshape((TOKENS, TOP))
    route_weights = jnp.clip(0.05 + 0.45 * jax.random.uniform(keys[3], (TOKENS, TOP), jnp.float32) ** levels(keys[3], (TOKENS, TOP), ((0, 32),), -0.2, 0.2), 0.05, 0.5)
    attn_gain = jnp.clip(1.0 + 0.1 * jax.random.normal(keys[4], (MODEL_WIDTH,), jnp.float32), 0.5, 1.5)
    mlp_gain = jnp.clip(1.0 + 0.1 * jax.random.normal(keys[5], (MODEL_WIDTH,), jnp.float32), 0.5, 1.5)
    joined_projection_weight = draw_joined_projection_weight(jax.random.fold_in(keys[12], 71), 0)
    output_weight = centred(keys[7], (MODEL_WIDTH, HQD), (MODEL_WIDTH // 32) ** -0.5, 1.0, ((0, 8), (1, 4)))
    w_gate = centred(keys[8], (E, MODEL_WIDTH, FF), MODEL_WIDTH ** -0.5, 0.1875, ((0, 8), (1, 4)))
    w_up = centred(keys[9], (E, MODEL_WIDTH, FF), MODEL_WIDTH ** -0.5, 0.1875, ((0, 8), (1, 4)))
    w_down = centred(keys[10], (E, FF, MODEL_WIDTH), (FF // 4) ** -0.5, 0.5, ((0, 8), (1, 4)))
    out_grad = draw_out_grad(jax.random.fold_in(keys[12], 71), 0)
    return dict(block_input=block_input, segment_ids=segment_ids, expert_routes=expert_routes, route_weights=route_weights, attn_gain=attn_gain, mlp_gain=mlp_gain, joined_projection_weight=joined_projection_weight, output_weight=output_weight, w_gate=w_gate, w_up=w_up, w_down=w_down, out_grad=out_grad)


EPS = 1e-06

def to_brain_float(values):
    return lax.optimization_barrier(values.astype(jnp.bfloat16))

def normalize(values, gains):
    scales = lax.rsqrt(lax.optimization_barrier(jnp.mean(values * values, axis=-1, keepdims=True)) + EPS)
    return (values * scales * gains, scales)

def norm_grad(values, scales, gains, upstream):
    unit_rows = values * scales
    inner_term = upstream * gains
    gain_part = lax.optimization_barrier(jnp.sum(upstream * unit_rows, axis=0))
    gradient = scales * (inner_term - unit_rows * lax.optimization_barrier(jnp.mean(inner_term * unit_rows, axis=-1, keepdims=True)))
    return (gradient, gain_part)

def rope_tables(segments):
    current = segments[:, :, None]
    earlier = segments[:, None, :]
    starts = lax.optimization_barrier(jnp.sum((earlier < current).astype(jnp.int32), axis=2))
    where_at = jnp.arange(segments.shape[1], dtype=jnp.int32)[None, :] - starts
    half_dim = HEAD_SIZE // 2
    frequency = jnp.exp(-math.log(10000.0) * jnp.arange(half_dim).astype(jnp.float32) / half_dim)
    angles = where_at.astype(jnp.float32)[..., None] * frequency
    return (jnp.cos(angles), jnp.sin(angles))

def rotate(values, cosine, sine_part):
    half_dim = values.shape[-1] // 2
    cos_wide = cosine[:, :, None, None, :]
    sin_wide = sine_part[:, :, None, None, :]
    first_half = values[..., :half_dim]
    second_half = values[..., half_dim:]
    return jnp.concatenate([first_half * cos_wide - second_half * sin_wide, second_half * cos_wide + first_half * sin_wide], axis=-1)

def unrotate(gradient, cosine, sine_part):
    half_dim = gradient.shape[-1] // 2
    cos_wide = cosine[:, :, None, None, :]
    sin_wide = sine_part[:, :, None, None, :]
    first_half = gradient[..., :half_dim]
    second_half = gradient[..., half_dim:]
    return jnp.concatenate([first_half * cos_wide + second_half * sin_wide, second_half * cos_wide - first_half * sin_wide], axis=-1)

def score_table(queries, key_rows, segments, scaling):
    raw_scores = jnp.einsum('pqgid,pkgd->pgiqk', queries.astype(jnp.float32), key_rows[..., 0, :].astype(jnp.float32)) * scaling
    same_doc = segments[:, :, None] == segments[:, None, :]
    ordering = jnp.arange(segments.shape[1])
    causal = ordering[None, :] <= ordering[:, None]
    allowed = (same_doc & causal[None])[:, None, None]
    return (jnp.where(allowed, raw_scores, -1e+30), allowed)

def attend_forward(queries, key_rows, value_rows, segments, scaling):
    scored, allowed = score_table(queries, key_rows, segments, scaling)
    row_max = lax.optimization_barrier(jnp.max(scored, axis=-1, keepdims=True))
    log_total = row_max + jnp.log(lax.optimization_barrier(jnp.sum(jnp.exp(scored - row_max), axis=-1, keepdims=True)))
    probability = jnp.where(allowed, jnp.exp(scored - log_total), 0.0)
    probs_low = to_brain_float(probability).astype(jnp.float32)
    result = jnp.einsum('pgiqk,pkgd->pqgid', probs_low, value_rows[..., 0, :].astype(jnp.float32))
    return (to_brain_float(result), log_total)

def attend_backward(queries, key_rows, value_rows, attention_result, heads_cotangent, log_total, segments, scaling):
    scored, allowed = score_table(queries, key_rows, segments, scaling)
    probability = jnp.where(allowed, jnp.exp(scored - log_total), 0.0)
    probs_low = to_brain_float(probability).astype(jnp.float32)
    cot_wide = heads_cotangent.astype(jnp.float32)
    value_gradient = jnp.einsum('pgiqk,pqgid->pkgd', probs_low, cot_wide)
    prob_grad = jnp.einsum('pqgid,pkgd->pgiqk', cot_wide, value_rows[..., 0, :].astype(jnp.float32))
    row_delta = jnp.einsum('pqgid,pqgid->pgiq', cot_wide, attention_result.astype(jnp.float32))[..., None]
    score_grad = to_brain_float(probability * (prob_grad - row_delta) * scaling).astype(jnp.float32)
    query_gradient = jnp.einsum('pgiqk,pkgd->pqgid', score_grad, key_rows[..., 0, :].astype(jnp.float32))
    key_gradient = jnp.einsum('pgiqk,pqgid->pkgd', score_grad, queries.astype(jnp.float32))
    return (query_gradient, key_gradient, value_gradient)

def slot_tables(route_block, weight_block):
    flattened = route_block.reshape(-1)
    matches = (flattened[:, None] == jnp.arange(E, dtype=jnp.int32)[None, :]).astype(jnp.int32)
    ranking = lax.optimization_barrier(jnp.sum((jnp.cumsum(matches, axis=0) - 1) * matches, axis=1))
    slot_of = flattened * CAP + ranking
    lookup = slot_of[None, :] == jnp.arange(E * CAP, dtype=jnp.int32)[:, None]
    filled = jnp.any(lookup, axis=1)
    token_index = jnp.arange(flattened.shape[0], dtype=jnp.int32) // route_block.shape[1]
    owner_tok = lax.optimization_barrier(jnp.sum(jnp.where(lookup, token_index[None, :], 0), axis=1)).astype(jnp.int32)
    weight = lax.optimization_barrier(jnp.sum(jnp.where(lookup, weight_block.reshape(-1)[None, :], 0.0), axis=1))
    return (slot_of.reshape(route_block.shape), filled, owner_tok, weight)

def reference(block_input, segment_ids, expert_routes, route_weights, attn_gain, mlp_gain, joined_projection_weight, output_weight, w_gate, w_up, w_down, out_grad):
    scaling = HEAD_SIZE ** (-0.5)
    attention_normed, attn_scale = normalize(block_input, attn_gain)
    attention_normed = to_brain_float(attention_normed)
    projected_rows = jnp.dot(attention_normed, joined_projection_weight, preferred_element_type=jnp.float32).reshape(PACKED_ROWS, PACKED_LENGTH, KEY_VALUE_HEADS, 4, HEAD_SIZE)
    cosine, sine_part = rope_tables(segment_ids)
    queries = to_brain_float(rotate(projected_rows[..., 0:2, :], cosine, sine_part))
    key_rows = to_brain_float(rotate(projected_rows[..., 2:3, :], cosine, sine_part))
    value_rows = to_brain_float(projected_rows[..., 3:4, :])

    def forward_pack(packed):
        return attend_forward(packed[0], packed[1], packed[2], packed[3], scaling)
    attention_result, log_total = lax.map(forward_pack, (queries[:, None], key_rows[:, None], value_rows[:, None], segment_ids[:, None]))
    attention_result = attention_result.reshape(PACKED_ROWS, PACKED_LENGTH, KEY_VALUE_HEADS, 2, HEAD_SIZE)
    heads_flat = attention_result.reshape(TOKENS, HQD)
    residual = block_input + jnp.dot(heads_flat, output_weight.T, preferred_element_type=jnp.float32)
    mlp_normed, mlp_scale = normalize(residual, mlp_gain)
    mlp_normed = to_brain_float(mlp_normed)
    blocks = TOKENS // TD
    slot_of, filled, owner_tok, weight = lax.map(lambda pair: slot_tables(pair[0], pair[1]), (expert_routes.reshape(blocks, TD, TOP), route_weights.reshape(blocks, TD, TOP)))
    owner_tok = owner_tok + (jnp.arange(blocks, dtype=jnp.int32) * TD)[:, None]
    owner_tok = owner_tok.reshape(blocks, E, CAP).transpose(1, 0, 2).reshape(E, blocks * CAP)
    filled = filled.reshape(blocks, E, CAP).transpose(1, 0, 2).reshape(E, blocks * CAP)
    weight = weight.reshape(blocks, E, CAP).transpose(1, 0, 2).reshape(E, blocks * CAP)

    def expert_step(carry, inputs):
        mixed, gathered_grad = carry
        gate_w_e, up_w_e, down_w_e, owner_e, filled_e, weight_e = inputs
        row_block = jnp.where(filled_e[:, None], mlp_normed[owner_e], 0).astype(jnp.bfloat16)
        gate_pre = jnp.dot(row_block, gate_w_e, preferred_element_type=jnp.float32)
        up_pre = jnp.dot(row_block, up_w_e, preferred_element_type=jnp.float32)
        sigmoid_gate = jax.nn.sigmoid(gate_pre)
        active = to_brain_float(gate_pre * sigmoid_gate * up_pre)
        produced = to_brain_float(jnp.dot(active, down_w_e, preferred_element_type=jnp.float32))
        mixed = mixed.at[owner_e].add(jnp.where(filled_e[:, None], weight_e[:, None] * produced.astype(jnp.float32), 0.0))
        expert_cot = to_brain_float(jnp.where(filled_e[:, None], weight_e[:, None] * out_grad[owner_e], 0.0))
        act_grad = jnp.dot(expert_cot, down_w_e.T, preferred_element_type=jnp.float32)
        down_grad = jnp.dot(active.T, expert_cot, preferred_element_type=jnp.float32)
        gate_grad = to_brain_float(act_grad * up_pre * sigmoid_gate * (1.0 + gate_pre * (1.0 - sigmoid_gate)))
        up_grad = to_brain_float(act_grad * gate_pre * sigmoid_gate)
        gate_w_grad = jnp.dot(row_block.T, gate_grad, preferred_element_type=jnp.float32)
        up_w_grad = jnp.dot(row_block.T, up_grad, preferred_element_type=jnp.float32)
        row_grad = to_brain_float(jnp.dot(gate_grad, gate_w_e.T, preferred_element_type=jnp.float32) + jnp.dot(up_grad, up_w_e.T, preferred_element_type=jnp.float32))
        gathered_grad = gathered_grad.at[owner_e].add(jnp.where(filled_e[:, None], row_grad.astype(jnp.float32), 0.0))
        return ((mixed, gathered_grad), (gate_w_grad, up_w_grad, down_grad))
    zeros_rows = jnp.zeros((TOKENS, MODEL_WIDTH), jnp.float32)
    carried, grads = lax.scan(expert_step, (zeros_rows, zeros_rows), (w_gate, w_up, w_down, owner_tok, filled, weight))
    mixed, mlp_normed_grad = carried
    w_gate_grad, w_up_grad, w_down_grad = grads
    block_output = residual + mixed
    residual_part, mlp_gain_grad = norm_grad(residual, mlp_scale, mlp_gain, mlp_normed_grad)
    residual_grad = out_grad + residual_part
    residual_cotangent = to_brain_float(residual_grad)
    w_out_grad = jnp.dot(residual_cotangent.T, heads_flat, preferred_element_type=jnp.float32)
    heads_cotangent = to_brain_float(jnp.dot(residual_cotangent, output_weight, preferred_element_type=jnp.float32)).reshape(PACKED_ROWS, PACKED_LENGTH, KEY_VALUE_HEADS, 2, HEAD_SIZE)

    def backward_pack(packed):
        return attend_backward(packed[0], packed[1], packed[2], packed[3], packed[4], packed[5], packed[6], scaling)
    query_gradient, key_gradient, value_gradient = lax.map(backward_pack, (queries[:, None], key_rows[:, None], value_rows[:, None], attention_result[:, None], heads_cotangent[:, None], log_total, segment_ids[:, None]))
    query_gradient = query_gradient.reshape(PACKED_ROWS, PACKED_LENGTH, KEY_VALUE_HEADS, 2, HEAD_SIZE)
    key_gradient = key_gradient.reshape(PACKED_ROWS, PACKED_LENGTH, KEY_VALUE_HEADS, 1, HEAD_SIZE)
    value_gradient = value_gradient.reshape(PACKED_ROWS, PACKED_LENGTH, KEY_VALUE_HEADS, 1, HEAD_SIZE)
    projected_grad = jnp.concatenate([unrotate(query_gradient, cosine, sine_part), unrotate(key_gradient, cosine, sine_part), value_gradient], axis=3)
    projected_grad = to_brain_float(projected_grad).reshape(TOKENS, QKV)
    w_qkv_grad = jnp.dot(attention_normed.T, projected_grad, preferred_element_type=jnp.float32)
    attn_normed_grad = jnp.dot(projected_grad, joined_projection_weight.T, preferred_element_type=jnp.float32)
    input_part, attn_gain_grad = norm_grad(block_input, attn_scale, attn_gain, attn_normed_grad)
    input_grad = residual_grad + input_part
    return (block_output, input_grad, attn_gain_grad, mlp_gain_grad, w_qkv_grad, w_out_grad, w_gate_grad, w_up_grad, w_down_grad)
```

```python
import math

import jax
import jax.numpy as jnp
from jax import lax
from jax.sharding import PartitionSpec as P

HEAD_SIZE = 64
E = 32
PACKED_LENGTH = 512
CAP = 36


EPS = 1e-06


def normalize(values, gains):
    scales = lax.rsqrt(jnp.mean(values * values, axis=-1, keepdims=True) + EPS)
    return (values * scales * gains, scales)


def norm_grad(values, scales, gains, upstream):
    unit_rows = values * scales
    inner_term = upstream * gains
    gain_part = jnp.sum(upstream * unit_rows, axis=0)
    gradient = scales * (
        inner_term - unit_rows * jnp.mean(inner_term * unit_rows, axis=-1, keepdims=True)
    )
    return (gradient, gain_part)


def rotary_tables(segments, width):
    current = segments[:, :, None]
    earlier = segments[:, None, :]
    starts = jnp.sum((earlier < current).astype(jnp.int32), axis=2)
    where_at = jnp.arange(segments.shape[1], dtype=jnp.int32)[None, :] - starts
    half_dim = HEAD_SIZE // 2
    column = jnp.arange(width, dtype=jnp.int32)
    within = column % HEAD_SIZE
    role_index = column // HEAD_SIZE % 4
    frequency = jnp.exp(-math.log(10000.0) * (within % half_dim).astype(jnp.float32) / half_dim)
    angles = where_at.reshape(-1).astype(jnp.float32)[:, None] * frequency[None, :]
    rotary = (role_index < 3)[None, :]
    first = (within < half_dim)[None, :]
    sine_full = jnp.sin(angles)
    cos_table = jnp.where(rotary, jnp.cos(angles), 1.0)
    sin_forward = jnp.where(rotary, jnp.where(first, -sine_full, sine_full), 0.0)
    same_block = column[:, None] // HEAD_SIZE == column[None, :] // HEAD_SIZE
    partner = column[:, None] % HEAD_SIZE == (within[None, :] + half_dim) % HEAD_SIZE
    swap_matrix = (same_block & partner).astype(jnp.float32)
    return (cos_table, sin_forward, swap_matrix)


def turn_rows(values, cos_table, sine_table, swap_matrix):
    swapped = jnp.dot(
        values, swap_matrix, precision=lax.Precision.HIGHEST, preferred_element_type=jnp.float32
    )
    return values * cos_table + swapped * sine_table


def allowed_table(segments):
    same_doc = segments[:, :, None] == segments[:, None, :]
    ordering = jnp.arange(segments.shape[1])
    causal = ordering[None, :] <= ordering[:, None]
    return same_doc & causal[None]


def head_slice(matrix, start, packs_here):
    return matrix[:, start : start + HEAD_SIZE].reshape(packs_here, PACKED_LENGTH, HEAD_SIZE)


def col_place():
    size = lax.axis_size("col")
    me = lax.axis_index("col")
    return size // 2, me // 2, me % 2


def col_shift(values, shift):
    size = lax.axis_size("col")
    pairs = [(i, (i // 2 - shift) % (size // 2) * 2 + i % 2) for i in range(size)]
    return lax.ppermute(values, "col", pairs)


def core_swap(values):
    size = lax.axis_size("col")
    return lax.ppermute(values, "col", [(i, i ^ 1) for i in range(size)])


def gather_parts(values):
    chips, _, _ = col_place()
    same = [values] + [col_shift(values, s) for s in range(1, chips)]
    return same + [core_swap(part) for part in same]


def part_owner(k):
    chips, chip, core = col_place()
    side = core if k < chips else 1 - core
    return (chip + k % chips) % chips * 2 + side


def gather_natural(values, axis):
    parts = gather_parts(values)
    size = values.shape[axis]
    shape = list(values.shape)
    shape[axis] = size * len(parts)
    whole = jnp.zeros(shape, values.dtype)
    for k, part in enumerate(parts):
        whole = lax.dynamic_update_slice_in_dim(whole, part, part_owner(k) * size, axis)
    return whole


def to_relative(values, axis):
    count = lax.axis_size("col")
    size = values.shape[axis] // count
    return jnp.concatenate(
        [
            lax.dynamic_slice_in_dim(values, part_owner(k) * size, size, axis)
            for k in range(count)
        ],
        axis=axis,
    )


def to_natural(values, axis):
    chips, chip, core = col_place()
    count = lax.axis_size("col")
    size = values.shape[axis] // count
    pieces = []
    for n in range(count):
        k = (n // 2 - chip) % chips + jnp.where(core == n % 2, 0, chips)
        pieces.append(lax.dynamic_slice_in_dim(values, k * size, size, axis))
    return jnp.concatenate(pieces, axis=axis)


def scatter_relative(values, axis):
    chips, _, _ = col_place()
    half = values.shape[axis] // 2
    size = half // chips
    other = lax.slice_in_dim(values, half, 2 * half, axis=axis).astype(jnp.bfloat16)
    arrived = core_swap(other)

    def part(k):
        mine = lax.slice_in_dim(values, k * size, (k + 1) * size, axis=axis)
        got = lax.slice_in_dim(arrived, k * size, (k + 1) * size, axis=axis)
        return mine.astype(jnp.float32) + got.astype(jnp.float32)

    total = part(0)
    for s in range(1, chips):
        total = total + col_shift(part(s).astype(jnp.bfloat16), chips - s).astype(jnp.float32)
    return total


def scatter_natural(values, axis, near=jnp.bfloat16):
    chips, chip, core = col_place()
    size = values.shape[axis] // (2 * chips)
    split = values.shape[:axis] + (chips, 2, size) + values.shape[axis + 1 :]
    split = values.reshape(split)
    other = lax.dynamic_index_in_dim(split, 1 - core, axis + 1, keepdims=False)
    mine = lax.dynamic_index_in_dim(split, core, axis + 1, keepdims=False)
    arrived = core_swap(other.astype(near))

    def part(s):
        at = (chip + s) % chips
        own = lax.dynamic_index_in_dim(mine, at, axis, keepdims=False)
        got = lax.dynamic_index_in_dim(arrived, at, axis, keepdims=False)
        return own.astype(jnp.float32) + got.astype(jnp.float32)

    total = part(0)
    for s in range(1, chips):
        total = total + col_shift(part(s).astype(jnp.bfloat16), chips - s).astype(jnp.float32)
    return total


def sum_everywhere(values):
    for name in ("col", "row"):
        size = lax.axis_size(name)
        step = 1
        while step < size:
            values = values + lax.ppermute(values, name, [(i, i ^ step) for i in range(size)])
            step *= 2
    return values


def slot_tables(routes, weights, experts, block):
    first = lax.axis_index("row") * experts
    wanted = (first + jnp.arange(experts, dtype=jnp.int32)).astype(jnp.float32)
    match = routes[:, :, None] == wanted[None, None, :]
    member = jnp.any(match, axis=1)
    weight = jnp.sum(jnp.where(match, weights[:, :, None], 0.0), axis=1)
    blocks = routes.shape[0] // block
    flags = member.astype(jnp.float32).reshape(blocks, block, experts)
    order = jnp.arange(block)
    earlier = (order[None, :] < order[:, None]).astype(jnp.float32)
    inside = jnp.einsum("ij,bje->bie", earlier, flags, preferred_element_type=jnp.float32)
    order = jnp.arange(blocks)
    before = (order[None, :] < order[:, None]).astype(jnp.float32)
    base = jnp.sum(before[:, :, None] * jnp.sum(flags, axis=1)[None], axis=1)
    rank = (inside + base[:, None, :]).reshape(-1, experts).astype(jnp.int32)
    slot = jnp.where(member, rank, -1).T
    slots = jnp.arange(blocks * CAP, dtype=jnp.int32)
    chosen = slot[:, None, :] == slots[None, :, None]
    slot_weight = jnp.sum(jnp.where(chosen, weight.T[:, None, :], 0.0), axis=2)
    return chosen.astype(jnp.bfloat16), slot_weight


def shards(
    block_input,
    segment_ids,
    expert_routes,
    route_weights,
    attn_gain,
    mlp_gain,
    joined_projection_weight,
    output_weight,
    w_gate,
    w_up,
    w_down,
    out_grad,
):
    scaling = HEAD_SIZE ** (-0.5)
    width = joined_projection_weight.shape[1]
    groups = width // (4 * HEAD_SIZE)
    packs_here = segment_ids.shape[0]
    row_count = packs_here * PACKED_LENGTH
    attention_normed, attn_scale = normalize(block_input, attn_gain)
    attention_normed = attention_normed.astype(jnp.bfloat16)
    normed_rows = gather_natural(attention_normed, 0)
    route_rows = lax.all_gather(
        jnp.concatenate([expert_routes.astype(jnp.float32), route_weights], axis=1),
        "row",
        axis=0,
        tiled=True,
    )
    picks = expert_routes.shape[1]
    experts = w_gate.shape[0]
    chosen, slot_weight = slot_tables(
        route_rows[:, :picks], route_rows[:, picks:], experts, block_input.shape[0]
    )
    pick_matrix = chosen.reshape(-1, chosen.shape[2])
    cot_rows_in = lax.all_gather(out_grad.astype(jnp.bfloat16), "row", axis=0, tiled=True)
    late_gate, late_up, late_down, normed_rows = lax.optimization_barrier(
        (w_gate, w_up, w_down, normed_rows)
    )
    gate_full = jnp.concatenate(gather_parts(late_gate), axis=1)
    up_full = jnp.concatenate(gather_parts(late_up), axis=1)
    down_full = gather_natural(late_down, 1)
    qkv_full, out_full = (
        lax.all_gather(joined_projection_weight, "row", axis=0, tiled=True),
        lax.all_gather(output_weight, "row", axis=0, tiled=True),
    )
    projected = jnp.dot(normed_rows, qkv_full, preferred_element_type=jnp.float32)
    cos_table, sin_forward, swap_matrix = rotary_tables(segment_ids, width)
    prepared = turn_rows(projected, cos_table, sin_forward, swap_matrix).astype(jnp.bfloat16)
    allowed = allowed_table(segment_ids)
    head_outputs = []
    log_totals = []
    for group in range(groups):
        base = group * 4 * HEAD_SIZE
        key_block = head_slice(prepared, base + 2 * HEAD_SIZE, packs_here)
        value_block = head_slice(prepared, base + 3 * HEAD_SIZE, packs_here)
        for inner in range(2):
            query_block = head_slice(prepared, base + inner * HEAD_SIZE, packs_here)
            scored = (
                jnp.einsum(
                    "pqd,pkd->pqk", query_block, key_block, preferred_element_type=jnp.float32
                )
                * scaling
            )
            scored = jnp.where(allowed, scored, -1e30)
            row_max = jnp.max(scored, axis=-1)
            log_total = row_max + jnp.log(jnp.sum(jnp.exp(scored - row_max[..., None]), axis=-1))
            probability = jnp.where(allowed, jnp.exp(scored - log_total[..., None]), 0.0).astype(
                jnp.bfloat16
            )
            result = jnp.einsum(
                "pqk,pkd->pqd", probability, value_block, preferred_element_type=jnp.float32
            ).astype(jnp.bfloat16)
            head_outputs.append(result.reshape(row_count, HEAD_SIZE))
            log_totals.append(log_total)
    heads_flat = jnp.concatenate(head_outputs, axis=1)
    row_block = heads_flat
    attention = scatter_natural(
        jnp.einsum("tj,dj->td", row_block, out_full, preferred_element_type=jnp.float32),
        0,
        jnp.float32,
    )
    residual = block_input + attention
    mlp_normed, mlp_scale = normalize(residual, mlp_gain)
    mlp_normed = mlp_normed.astype(jnp.bfloat16)
    token_rows = lax.all_gather(to_relative(mlp_normed, 1), "row", axis=0, tiled=True)

    def to_slots(rows):
        return jnp.dot(pick_matrix, rows, preferred_element_type=jnp.float32)

    def to_tokens(rows):
        partial = lax.dot_general(
            pick_matrix,
            rows.reshape(pick_matrix.shape[0], -1),
            (((0,), (0,)), ((), ())),
            preferred_element_type=jnp.float32,
        ).astype(jnp.bfloat16)
        return lax.psum_scatter(partial, "row", scatter_dimension=0, tiled=True).astype(
            jnp.float32
        )

    cot_arrived = (
        (to_slots(cot_rows_in) * slot_weight.reshape(-1, 1))
        .astype(jnp.bfloat16)
        .reshape(experts, -1, cot_rows_in.shape[1])
    )
    act_grad = jnp.einsum(
        "erd,efd->erf", cot_arrived, down_full, preferred_element_type=jnp.float32
    )
    arrived = to_slots(token_rows).astype(jnp.bfloat16).reshape(cot_arrived.shape)
    gate_pre = jnp.einsum("erd,edf->erf", arrived, gate_full, preferred_element_type=jnp.float32)
    up_pre = jnp.einsum("erd,edf->erf", arrived, up_full, preferred_element_type=jnp.float32)
    sigmoid_gate = jax.nn.sigmoid(gate_pre)
    active = (gate_pre * sigmoid_gate * up_pre).astype(jnp.bfloat16)
    gate_grad = (act_grad * up_pre * sigmoid_gate * (1.0 + gate_pre * (1.0 - sigmoid_gate))).astype(
        jnp.bfloat16
    )
    up_grad = (act_grad * gate_pre * sigmoid_gate).astype(jnp.bfloat16)
    row_grad = jnp.einsum("erf,edf->erd", gate_grad, gate_full, preferred_element_type=jnp.float32)
    row_grad = (
        row_grad + jnp.einsum("erf,edf->erd", up_grad, up_full, preferred_element_type=jnp.float32)
    ).astype(jnp.bfloat16)
    mlp_normed_grad = to_natural(to_tokens(row_grad), 1)
    gate_w_grad = jnp.einsum(
        "erd,erf->edf", arrived, gate_grad, preferred_element_type=jnp.float32
    ).astype(jnp.bfloat16)
    up_w_grad = jnp.einsum(
        "erd,erf->edf", arrived, up_grad, preferred_element_type=jnp.float32
    ).astype(jnp.bfloat16)
    down_grad = jnp.einsum(
        "erf,erd->efd", active, cot_arrived, preferred_element_type=jnp.float32
    ).astype(jnp.bfloat16)
    gate_share = scatter_relative(gate_w_grad, 1)
    up_share = scatter_relative(up_w_grad, 1)
    down_share = scatter_natural(down_grad, 1)
    produced = (
        jnp.einsum("erf,efd->erd", active, down_full, preferred_element_type=jnp.float32)
        * slot_weight[..., None]
    ).astype(jnp.bfloat16)
    block_output = residual + to_tokens(produced)
    residual_part, mlp_part = norm_grad(residual, mlp_scale, mlp_gain, mlp_normed_grad)
    residual_grad = out_grad + residual_part
    residual_cotangent = residual_grad.astype(jnp.bfloat16)
    cot_rows = gather_natural(residual_cotangent, 0)
    heads_cotangent = jnp.einsum(
        "td,dj->tj", cot_rows, out_full, preferred_element_type=jnp.float32
    ).astype(jnp.bfloat16)
    out_grad_part = jnp.einsum(
        "td,tj->dj", cot_rows, heads_flat, preferred_element_type=jnp.float32
    )
    grad_pieces = []
    for group in range(groups):
        base = group * 4 * HEAD_SIZE
        key_block = head_slice(prepared, base + 2 * HEAD_SIZE, packs_here)
        value_block = head_slice(prepared, base + 3 * HEAD_SIZE, packs_here)
        key_gradient = jnp.zeros((packs_here, PACKED_LENGTH, HEAD_SIZE), jnp.float32)
        value_gradient = jnp.zeros((packs_here, PACKED_LENGTH, HEAD_SIZE), jnp.float32)
        query_parts = []
        for inner in range(2):
            head_number = 2 * group + inner
            query_block = head_slice(prepared, base + inner * HEAD_SIZE, packs_here)
            cot_block = head_slice(heads_cotangent, head_number * HEAD_SIZE, packs_here)
            result_block = head_slice(heads_flat, head_number * HEAD_SIZE, packs_here)
            scored = (
                jnp.einsum(
                    "pqd,pkd->pqk", query_block, key_block, preferred_element_type=jnp.float32
                )
                * scaling
            )
            scored = jnp.where(allowed, scored, -1e30)
            probability = jnp.where(
                allowed, jnp.exp(scored - log_totals[head_number][..., None]), 0.0
            )
            value_gradient = value_gradient + jnp.einsum(
                "pqk,pqd->pkd",
                probability.astype(jnp.bfloat16),
                cot_block,
                preferred_element_type=jnp.float32,
            )
            prob_grad = jnp.einsum(
                "pqd,pkd->pqk", cot_block, value_block, preferred_element_type=jnp.float32
            )
            row_delta = jnp.einsum(
                "pqd,pqd->pq", cot_block, result_block, preferred_element_type=jnp.float32
            )
            score_grad = (probability * (prob_grad - row_delta[..., None]) * scaling).astype(
                jnp.bfloat16
            )
            query_parts.append(
                jnp.einsum(
                    "pqk,pkd->pqd", score_grad, key_block, preferred_element_type=jnp.float32
                ).reshape(row_count, HEAD_SIZE)
            )
            key_gradient = key_gradient + jnp.einsum(
                "pqk,pqd->pkd", score_grad, query_block, preferred_element_type=jnp.float32
            )
        grad_pieces.extend(query_parts)
        grad_pieces.append(key_gradient.reshape(row_count, HEAD_SIZE))
        grad_pieces.append(value_gradient.reshape(row_count, HEAD_SIZE))
    raw_grad = jnp.concatenate(grad_pieces, axis=1)
    projected_grad = turn_rows(raw_grad, cos_table, -sin_forward, swap_matrix).astype(jnp.bfloat16)
    qkv_grad_part = jnp.einsum(
        "td,tj->dj", normed_rows, projected_grad, preferred_element_type=jnp.float32
    )
    qkv_share, out_share = (
        lax.psum_scatter(
            qkv_grad_part.astype(jnp.bfloat16), "row", scatter_dimension=0, tiled=True
        ).astype(jnp.float32),
        lax.psum_scatter(
            out_grad_part.astype(jnp.bfloat16), "row", scatter_dimension=0, tiled=True
        ).astype(jnp.float32),
    )
    row_block = projected_grad
    attn_normed_grad = scatter_natural(
        jnp.einsum("tj,dj->td", row_block, qkv_full, preferred_element_type=jnp.float32),
        0,
        jnp.float32,
    )
    input_part, attn_part = norm_grad(block_input, attn_scale, attn_gain, attn_normed_grad)
    input_grad = residual_grad + input_part
    attn_gain_grad, mlp_gain_grad = sum_everywhere(jnp.stack([attn_part, mlp_part]))
    return (
        block_output,
        input_grad,
        attn_gain_grad,
        mlp_gain_grad,
        qkv_share,
        out_share,
        gate_share,
        up_share,
        down_share,
    )


def solution(mesh):
    in_specs = (
        P(("row", "col"), None),
        P("row", None),
        P(("row", "col"), None),
        P(("row", "col"), None),
        P(),
        P(),
        P("row", "col"),
        P("row", "col"),
        P("row", "col", None),
        P("row", "col", None),
        P("row", "col", None),
        P(("row", "col"), None),
    )
    out_specs = (
        P(("row", "col"), None),
        P(("row", "col"), None),
        P(),
        P(),
        P("row", "col"),
        P("row", "col"),
        P("row", "col", None),
        P("row", "col", None),
        P("row", "col", None),
    )
    return jax.shard_map(shards, mesh=mesh, in_specs=in_specs, out_specs=out_specs, check_vma=False)
```

```python
import math

import jax
import jax.numpy as jnp
from jax import lax
from jax.sharding import PartitionSpec as P

HEAD_SIZE = 64
E = 32
PACKED_LENGTH = 512
CAP = 36


EPS = 1e-06


def normalize(values, gains):
    scales = lax.rsqrt(jnp.mean(values * values, axis=-1, keepdims=True) + EPS)
    return (values * scales * gains, scales)


def norm_grad(values, scales, gains, upstream):
    unit_rows = values * scales
    inner_term = upstream * gains
    gain_part = jnp.sum(upstream * unit_rows, axis=0)
    gradient = scales * (
        inner_term - unit_rows * jnp.mean(inner_term * unit_rows, axis=-1, keepdims=True)
    )
    return (gradient, gain_part)


def rotary_tables(segments, width):
    current = segments[:, :, None]
    earlier = segments[:, None, :]
    starts = jnp.sum((earlier < current).astype(jnp.int32), axis=2)
    where_at = jnp.arange(segments.shape[1], dtype=jnp.int32)[None, :] - starts
    half_dim = HEAD_SIZE // 2
    column = jnp.arange(width, dtype=jnp.int32)
    within = column % HEAD_SIZE
    role_index = column // HEAD_SIZE % 4
    frequency = jnp.exp(-math.log(10000.0) * (within % half_dim).astype(jnp.float32) / half_dim)
    angles = where_at.reshape(-1).astype(jnp.float32)[:, None] * frequency[None, :]
    rotary = (role_index < 3)[None, :]
    first = (within < half_dim)[None, :]
    sine_full = jnp.sin(angles)
    cos_table = jnp.where(rotary, jnp.cos(angles), 1.0)
    sin_forward = jnp.where(rotary, jnp.where(first, -sine_full, sine_full), 0.0)
    same_block = column[:, None] // HEAD_SIZE == column[None, :] // HEAD_SIZE
    partner = column[:, None] % HEAD_SIZE == (within[None, :] + half_dim) % HEAD_SIZE
    swap_matrix = (same_block & partner).astype(jnp.float32)
    return (cos_table, sin_forward, swap_matrix)


def turn_rows(values, cos_table, sine_table, swap_matrix):
    swapped = jnp.dot(
        values, swap_matrix, precision=lax.Precision.HIGHEST, preferred_element_type=jnp.float32
    )
    return values * cos_table + swapped * sine_table


def allowed_table(segments):
    same_doc = segments[:, :, None] == segments[:, None, :]
    ordering = jnp.arange(segments.shape[1])
    causal = ordering[None, :] <= ordering[:, None]
    return same_doc & causal[None]


def head_slice(matrix, start, packs_here):
    return matrix[:, start : start + HEAD_SIZE].reshape(packs_here, PACKED_LENGTH, HEAD_SIZE)


def col_place():
    size = lax.axis_size("col")
    me = lax.axis_index("col")
    return size // 2, me // 2, me % 2


def col_shift(values, shift):
    size = lax.axis_size("col")
    pairs = [(i, (i // 2 - shift) % (size // 2) * 2 + i % 2) for i in range(size)]
    return lax.ppermute(values, "col", pairs)


def core_swap(values):
    size = lax.axis_size("col")
    return lax.ppermute(values, "col", [(i, i ^ 1) for i in range(size)])


def chip_parts(values):
    chips, _, _ = col_place()
    return [values] + [col_shift(values, s) for s in range(1, chips)]


def gather_parts(values):
    same = chip_parts(values)
    return same + [core_swap(part) for part in same]


def part_owner(k):
    chips, chip, core = col_place()
    side = core if k < chips else 1 - core
    return (chip + k % chips) % chips * 2 + side


def gather_natural(values, axis):
    parts = gather_parts(values)
    size = values.shape[axis]
    shape = list(values.shape)
    shape[axis] = size * len(parts)
    whole = jnp.zeros(shape, values.dtype)
    for k, part in enumerate(parts):
        whole = lax.dynamic_update_slice_in_dim(whole, part, part_owner(k) * size, axis)
    return whole


def to_relative(values, axis):
    count = lax.axis_size("col")
    size = values.shape[axis] // count
    return jnp.concatenate(
        [
            lax.dynamic_slice_in_dim(values, part_owner(k) * size, size, axis)
            for k in range(count)
        ],
        axis=axis,
    )


def to_natural(values, axis):
    chips, chip, core = col_place()
    count = lax.axis_size("col")
    size = values.shape[axis] // count
    pieces = []
    for n in range(count):
        k = (n // 2 - chip) % chips + jnp.where(core == n % 2, 0, chips)
        pieces.append(lax.dynamic_slice_in_dim(values, k * size, size, axis))
    return jnp.concatenate(pieces, axis=axis)


def near_relative(values, axis):
    half = values.shape[axis] // 2
    other = lax.slice_in_dim(values, half, 2 * half, axis=axis).astype(jnp.bfloat16)
    mine = lax.slice_in_dim(values, 0, half, axis=axis)
    total = mine.astype(jnp.float32) + core_swap(other).astype(jnp.float32)
    return total.astype(jnp.bfloat16)


def far_relative(values, axis):
    chips, _, _ = col_place()
    size = values.shape[axis] // chips
    parts = [lax.slice_in_dim(values, k * size, (k + 1) * size, axis=axis) for k in range(chips)]
    total = parts[0].astype(jnp.float32)
    for s in range(1, chips):
        total = total + col_shift(parts[s], chips - s).astype(jnp.float32)
    return total


def near_natural(values, axis, near):
    chips, _, core = col_place()
    size = values.shape[axis] // (2 * chips)
    split = values.shape[:axis] + (chips, 2, size) + values.shape[axis + 1 :]
    split = values.reshape(split)
    other = lax.dynamic_index_in_dim(split, 1 - core, axis + 1, keepdims=False)
    mine = lax.dynamic_index_in_dim(split, core, axis + 1, keepdims=False)
    return mine.astype(jnp.float32) + core_swap(other.astype(near)).astype(jnp.float32)


def far_natural(values, axis):
    chips, chip, _ = col_place()

    def part(s):
        return lax.dynamic_index_in_dim(values, (chip + s) % chips, axis, keepdims=False)

    total = part(0).astype(jnp.float32)
    for s in range(1, chips):
        total = total + col_shift(part(s).astype(jnp.bfloat16), chips - s).astype(jnp.float32)
    return total


def scatter_natural(values, axis, near):
    return far_natural(near_natural(values, axis, near), axis)


def row_gather(values, axis):
    size = lax.axis_size("row")
    me = lax.axis_index("row")
    step = 1
    while step < size:
        got = lax.ppermute(values, "row", [(i, i ^ step) for i in range(size)])
        upper = (me // step) % 2 == 1
        values = jnp.concatenate(
            [jnp.where(upper, got, values), jnp.where(upper, values, got)], axis=axis
        )
        step *= 2
    return values


def row_scatter(values):
    size = lax.axis_size("row")
    parts = values.reshape(size, values.shape[0] // size, values.shape[1])
    parts = lax.all_to_all(parts, "row", split_axis=0, concat_axis=0, tiled=True)
    return jnp.sum(parts.astype(jnp.float32), axis=0)


def sum_everywhere(values):
    for name in ("col", "row"):
        size = lax.axis_size(name)
        step = 1
        while step < size:
            values = values + lax.ppermute(values, name, [(i, i ^ step) for i in range(size)])
            step *= 2
    return values


def slot_tables(routes, weights, experts, block):
    first = lax.axis_index("row") * experts
    wanted = (first + jnp.arange(experts, dtype=jnp.int32)).astype(jnp.float32)
    match = routes[:, :, None] == wanted[None, None, :]
    member = jnp.any(match, axis=1)
    weight = jnp.sum(jnp.where(match, weights[:, :, None], 0.0), axis=1)
    blocks = routes.shape[0] // block
    flags = member.astype(jnp.float32).reshape(blocks, block, experts)
    order = jnp.arange(block)
    earlier = (order[None, :] < order[:, None]).astype(jnp.float32)
    inside = jnp.einsum("ij,bje->bie", earlier, flags, preferred_element_type=jnp.float32)
    order = jnp.arange(blocks)
    before = (order[None, :] < order[:, None]).astype(jnp.float32)
    base = jnp.sum(before[:, :, None] * jnp.sum(flags, axis=1)[None], axis=1)
    rank = (inside + base[:, None, :]).reshape(-1, experts).astype(jnp.int32)
    slot = jnp.where(member, rank, -1).T
    slots = jnp.arange(blocks * CAP, dtype=jnp.int32)
    chosen = slot[:, None, :] == slots[None, :, None]
    slot_weight = jnp.sum(jnp.where(chosen, weight.T[:, None, :], 0.0), axis=2)
    return chosen.astype(jnp.bfloat16), slot_weight


def shards(
    block_input,
    segment_ids,
    expert_routes,
    route_weights,
    attn_gain,
    mlp_gain,
    joined_projection_weight,
    output_weight,
    w_gate,
    w_up,
    w_down,
    out_grad,
):
    scaling = HEAD_SIZE ** (-0.5)
    width = joined_projection_weight.shape[1]
    groups = width // (4 * HEAD_SIZE)
    packs_here = segment_ids.shape[0]
    row_count = packs_here * PACKED_LENGTH
    attention_normed, attn_scale = normalize(block_input, attn_gain)
    attention_normed = attention_normed.astype(jnp.bfloat16)
    normed_rows = gather_natural(attention_normed, 0)
    route_rows = row_gather(
        jnp.concatenate([expert_routes.astype(jnp.float32), route_weights], axis=1).T, 1
    ).T
    picks = expert_routes.shape[1]
    experts = w_gate.shape[0]
    chosen, slot_weight = slot_tables(
        route_rows[:, :picks], route_rows[:, picks:], experts, block_input.shape[0]
    )
    pick_matrix = chosen.reshape(-1, chosen.shape[2])
    gate_parts = chip_parts(w_gate)
    up_parts = chip_parts(w_up)
    gate_parts, up_parts, normed_rows, pick_matrix, slot_weight, w_down = lax.optimization_barrier(
        (gate_parts, up_parts, normed_rows, pick_matrix, slot_weight, w_down)
    )
    gate_full = jnp.concatenate(gate_parts + [core_swap(part) for part in gate_parts], axis=1)
    up_full = jnp.concatenate(up_parts + [core_swap(part) for part in up_parts], axis=1)
    down_full = gather_natural(w_down, 1)
    joined = lax.all_gather(
        jnp.concatenate([joined_projection_weight, output_weight], axis=1),
        "row",
        axis=0,
        tiled=True,
    )
    late_out_grad, joined = lax.optimization_barrier((out_grad.astype(jnp.bfloat16), joined))
    qkv_full, out_full = joined[:, :width], joined[:, width:]
    cot_rows_in = row_gather(late_out_grad, 0)
    projected = jnp.dot(normed_rows, qkv_full, preferred_element_type=jnp.float32)
    cos_table, sin_forward, swap_matrix = rotary_tables(segment_ids, width)
    prepared = turn_rows(projected, cos_table, sin_forward, swap_matrix).astype(jnp.bfloat16)
    allowed = allowed_table(segment_ids)
    head_outputs = []
    log_totals = []
    for group in range(groups):
        base = group * 4 * HEAD_SIZE
        key_block = head_slice(prepared, base + 2 * HEAD_SIZE, packs_here)
        value_block = head_slice(prepared, base + 3 * HEAD_SIZE, packs_here)
        for inner in range(2):
            query_block = head_slice(prepared, base + inner * HEAD_SIZE, packs_here)
            scored = (
                jnp.einsum(
                    "pqd,pkd->pqk", query_block, key_block, preferred_element_type=jnp.float32
                )
                * scaling
            )
            scored = jnp.where(allowed, scored, -1e30)
            row_max = jnp.max(scored, axis=-1)
            log_total = row_max + jnp.log(jnp.sum(jnp.exp(scored - row_max[..., None]), axis=-1))
            probability = jnp.where(allowed, jnp.exp(scored - log_total[..., None]), 0.0).astype(
                jnp.bfloat16
            )
            result = jnp.einsum(
                "pqk,pkd->pqd", probability, value_block, preferred_element_type=jnp.float32
            ).astype(jnp.bfloat16)
            head_outputs.append(result.reshape(row_count, HEAD_SIZE))
            log_totals.append(log_total)
    heads_flat = jnp.concatenate(head_outputs, axis=1)
    row_block = heads_flat
    attention = scatter_natural(
        jnp.einsum("tj,dj->td", row_block, out_full, preferred_element_type=jnp.float32),
        0,
        jnp.float32,
    )
    residual = block_input + attention
    mlp_normed, mlp_scale = normalize(residual, mlp_gain)
    mlp_normed = mlp_normed.astype(jnp.bfloat16)
    token_rows = lax.all_gather(to_relative(mlp_normed, 1), "row", axis=0, tiled=True)

    def to_slots(rows):
        return jnp.dot(pick_matrix, rows, preferred_element_type=jnp.float32)

    def to_tokens(rows):
        return lax.dot_general(
            pick_matrix,
            rows.reshape(pick_matrix.shape[0], -1),
            (((0,), (0,)), ((), ())),
            preferred_element_type=jnp.float32,
        ).astype(jnp.bfloat16)

    cot_arrived = (
        (to_slots(cot_rows_in) * slot_weight.reshape(-1, 1))
        .astype(jnp.bfloat16)
        .reshape(experts, -1, cot_rows_in.shape[1])
    )
    act_grad = jnp.einsum(
        "erd,efd->erf", cot_arrived, down_full, preferred_element_type=jnp.float32
    )
    arrived = to_slots(token_rows).astype(jnp.bfloat16).reshape(cot_arrived.shape)
    gate_pre = jnp.einsum("erd,edf->erf", arrived, gate_full, preferred_element_type=jnp.float32)
    up_pre = jnp.einsum("erd,edf->erf", arrived, up_full, preferred_element_type=jnp.float32)
    sigmoid_gate = jax.nn.sigmoid(gate_pre)
    active = (gate_pre * sigmoid_gate * up_pre).astype(jnp.bfloat16)
    gate_grad = (act_grad * up_pre * sigmoid_gate * (1.0 + gate_pre * (1.0 - sigmoid_gate))).astype(
        jnp.bfloat16
    )
    up_grad = (act_grad * gate_pre * sigmoid_gate).astype(jnp.bfloat16)
    row_grad = jnp.einsum("erf,edf->erd", gate_grad, gate_full, preferred_element_type=jnp.float32)
    row_grad = (
        row_grad + jnp.einsum("erf,edf->erd", up_grad, up_full, preferred_element_type=jnp.float32)
    ).astype(jnp.bfloat16)
    mlp_normed_grad = to_natural(row_scatter(to_tokens(row_grad)), 1)
    gate_w_grad = jnp.einsum(
        "erd,erf->edf", arrived, gate_grad, preferred_element_type=jnp.float32
    ).astype(jnp.bfloat16)
    up_w_grad = jnp.einsum(
        "erd,erf->edf", arrived, up_grad, preferred_element_type=jnp.float32
    ).astype(jnp.bfloat16)
    down_grad = jnp.einsum(
        "erf,erd->efd", active, cot_arrived, preferred_element_type=jnp.float32
    ).astype(jnp.bfloat16)
    produced = (
        jnp.einsum("erf,efd->erd", active, down_full, preferred_element_type=jnp.float32)
        * slot_weight[..., None]
    ).astype(jnp.bfloat16)
    produced_rows = to_tokens(produced)
    gate_share = far_relative(near_relative(gate_w_grad, 1), 1)
    up_share = far_relative(near_relative(up_w_grad, 1), 1)
    down_near = near_natural(down_grad, 1, jnp.bfloat16).astype(jnp.bfloat16)
    mlp_normed_grad, produced_rows, gate_share, up_share, down_near = lax.optimization_barrier(
        (mlp_normed_grad, produced_rows, gate_share, up_share, down_near)
    )
    down_share = far_natural(down_near, 1)
    block_output = residual + lax.psum_scatter(
        produced_rows, "row", scatter_dimension=0, tiled=True
    ).astype(jnp.float32)
    residual_part, mlp_part = norm_grad(residual, mlp_scale, mlp_gain, mlp_normed_grad)
    residual_grad = out_grad + residual_part
    residual_cotangent = residual_grad.astype(jnp.bfloat16)
    cot_rows = gather_natural(residual_cotangent, 0)
    heads_cotangent = jnp.einsum(
        "td,dj->tj", cot_rows, out_full, preferred_element_type=jnp.float32
    ).astype(jnp.bfloat16)
    out_grad_part = jnp.einsum(
        "td,tj->dj", cot_rows, heads_flat, preferred_element_type=jnp.float32
    )
    grad_pieces = []
    for group in range(groups):
        base = group * 4 * HEAD_SIZE
        key_block = head_slice(prepared, base + 2 * HEAD_SIZE, packs_here)
        value_block = head_slice(prepared, base + 3 * HEAD_SIZE, packs_here)
        key_gradient = jnp.zeros((packs_here, PACKED_LENGTH, HEAD_SIZE), jnp.float32)
        value_gradient = jnp.zeros((packs_here, PACKED_LENGTH, HEAD_SIZE), jnp.float32)
        query_parts = []
        for inner in range(2):
            head_number = 2 * group + inner
            query_block = head_slice(prepared, base + inner * HEAD_SIZE, packs_here)
            cot_block = head_slice(heads_cotangent, head_number * HEAD_SIZE, packs_here)
            result_block = head_slice(heads_flat, head_number * HEAD_SIZE, packs_here)
            scored = (
                jnp.einsum(
                    "pqd,pkd->pqk", query_block, key_block, preferred_element_type=jnp.float32
                )
                * scaling
            )
            scored = jnp.where(allowed, scored, -1e30)
            probability = jnp.where(
                allowed, jnp.exp(scored - log_totals[head_number][..., None]), 0.0
            )
            value_gradient = value_gradient + jnp.einsum(
                "pqk,pqd->pkd",
                probability.astype(jnp.bfloat16),
                cot_block,
                preferred_element_type=jnp.float32,
            )
            prob_grad = jnp.einsum(
                "pqd,pkd->pqk", cot_block, value_block, preferred_element_type=jnp.float32
            )
            row_delta = jnp.einsum(
                "pqd,pqd->pq", cot_block, result_block, preferred_element_type=jnp.float32
            )
            score_grad = (probability * (prob_grad - row_delta[..., None]) * scaling).astype(
                jnp.bfloat16
            )
            query_parts.append(
                jnp.einsum(
                    "pqk,pkd->pqd", score_grad, key_block, preferred_element_type=jnp.float32
                ).reshape(row_count, HEAD_SIZE)
            )
            key_gradient = key_gradient + jnp.einsum(
                "pqk,pqd->pkd", score_grad, query_block, preferred_element_type=jnp.float32
            )
        grad_pieces.extend(query_parts)
        grad_pieces.append(key_gradient.reshape(row_count, HEAD_SIZE))
        grad_pieces.append(value_gradient.reshape(row_count, HEAD_SIZE))
    raw_grad = jnp.concatenate(grad_pieces, axis=1)
    projected_grad = turn_rows(raw_grad, cos_table, -sin_forward, swap_matrix).astype(jnp.bfloat16)
    qkv_grad_part = jnp.einsum(
        "td,tj->dj", normed_rows, projected_grad, preferred_element_type=jnp.float32
    )
    qkv_share = row_scatter(qkv_grad_part.astype(jnp.bfloat16))
    out_share = row_scatter(out_grad_part.astype(jnp.bfloat16))
    row_block = projected_grad
    attn_normed_grad = scatter_natural(
        jnp.einsum("tj,dj->td", row_block, qkv_full, preferred_element_type=jnp.float32),
        0,
        jnp.float32,
    )
    input_part, attn_part = norm_grad(block_input, attn_scale, attn_gain, attn_normed_grad)
    input_grad = residual_grad + input_part
    attn_gain_grad, mlp_gain_grad = sum_everywhere(jnp.stack([attn_part, mlp_part]))
    return (
        block_output,
        input_grad,
        attn_gain_grad,
        mlp_gain_grad,
        qkv_share,
        out_share,
        gate_share,
        up_share,
        down_share,
    )


def solution(mesh):
    in_specs = (
        P(("row", "col"), None),
        P("row", None),
        P(("row", "col"), None),
        P(("row", "col"), None),
        P(),
        P(),
        P("row", "col"),
        P("row", "col"),
        P("row", "col", None),
        P("row", "col", None),
        P("row", "col", None),
        P(("row", "col"), None),
    )
    out_specs = (
        P(("row", "col"), None),
        P(("row", "col"), None),
        P(),
        P(),
        P("row", "col"),
        P("row", "col"),
        P("row", "col", None),
        P("row", "col", None),
        P("row", "col", None),
    )
    return jax.shard_map(shards, mesh=mesh, in_specs=in_specs, out_specs=out_specs, check_vma=False)
```

```python
import math

import jax
import jax.numpy as jnp
from jax import lax
from jax.sharding import PartitionSpec as P

HEAD_SIZE = 64
E = 32
PACKED_LENGTH = 512
CAP = 36


EPS = 1e-06


def normalize(values, gains):
    scales = lax.rsqrt(jnp.mean(values * values, axis=-1, keepdims=True) + EPS)
    return (values * scales * gains, scales)


def norm_grad(values, scales, gains, upstream):
    unit_rows = values * scales
    inner_term = upstream * gains
    gain_part = jnp.sum(upstream * unit_rows, axis=0)
    gradient = scales * (
        inner_term - unit_rows * jnp.mean(inner_term * unit_rows, axis=-1, keepdims=True)
    )
    return (gradient, gain_part)


def rotary_tables(segments, width):
    current = segments[:, :, None]
    earlier = segments[:, None, :]
    starts = jnp.sum((earlier < current).astype(jnp.int32), axis=2)
    where_at = jnp.arange(segments.shape[1], dtype=jnp.int32)[None, :] - starts
    half_dim = HEAD_SIZE // 2
    column = jnp.arange(width, dtype=jnp.int32)
    within = column % HEAD_SIZE
    role_index = column // HEAD_SIZE % 4
    frequency = jnp.exp(-math.log(10000.0) * (within % half_dim).astype(jnp.float32) / half_dim)
    angles = where_at.reshape(-1).astype(jnp.float32)[:, None] * frequency[None, :]
    rotary = (role_index < 3)[None, :]
    first = (within < half_dim)[None, :]
    sine_full = jnp.sin(angles)
    cos_table = jnp.where(rotary, jnp.cos(angles), 1.0)
    sin_forward = jnp.where(rotary, jnp.where(first, -sine_full, sine_full), 0.0)
    same_block = column[:, None] // HEAD_SIZE == column[None, :] // HEAD_SIZE
    partner = column[:, None] % HEAD_SIZE == (within[None, :] + half_dim) % HEAD_SIZE
    swap_matrix = (same_block & partner).astype(jnp.float32)
    return (cos_table, sin_forward, swap_matrix)


def turn_rows(values, cos_table, sine_table, swap_matrix):
    swapped = jnp.dot(
        values, swap_matrix, precision=lax.Precision.HIGHEST, preferred_element_type=jnp.float32
    )
    return values * cos_table + swapped * sine_table


def allowed_table(segments):
    same_doc = segments[:, :, None] == segments[:, None, :]
    ordering = jnp.arange(segments.shape[1])
    causal = ordering[None, :] <= ordering[:, None]
    return same_doc & causal[None]


def head_slice(matrix, start, packs_here):
    return matrix[:, start : start + HEAD_SIZE].reshape(packs_here, PACKED_LENGTH, HEAD_SIZE)


def col_place():
    size = lax.axis_size("col")
    me = lax.axis_index("col")
    return size // 2, me // 2, me % 2


def col_shift(values, shift):
    size = lax.axis_size("col")
    pairs = [(i, (i // 2 - shift) % (size // 2) * 2 + i % 2) for i in range(size)]
    return lax.ppermute(values, "col", pairs)


def core_swap(values):
    size = lax.axis_size("col")
    return lax.ppermute(values, "col", [(i, i ^ 1) for i in range(size)])


def chip_parts(values):
    chips, _, _ = col_place()
    return [values] + [col_shift(values, s) for s in range(1, chips)]


def gather_parts(values):
    same = chip_parts(values)
    return same + [core_swap(part) for part in same]


def part_owner(k):
    chips, chip, core = col_place()
    side = core if k < chips else 1 - core
    return (chip + k % chips) % chips * 2 + side


def gather_natural(values, axis):
    parts = gather_parts(values)
    size = values.shape[axis]
    shape = list(values.shape)
    shape[axis] = size * len(parts)
    whole = jnp.zeros(shape, values.dtype)
    for k, part in enumerate(parts):
        whole = lax.dynamic_update_slice_in_dim(whole, part, part_owner(k) * size, axis)
    return whole


def to_relative(values, axis):
    count = lax.axis_size("col")
    size = values.shape[axis] // count
    return jnp.concatenate(
        [
            lax.dynamic_slice_in_dim(values, part_owner(k) * size, size, axis)
            for k in range(count)
        ],
        axis=axis,
    )


def to_natural(values, axis):
    chips, chip, core = col_place()
    count = lax.axis_size("col")
    size = values.shape[axis] // count
    pieces = []
    for n in range(count):
        k = (n // 2 - chip) % chips + jnp.where(core == n % 2, 0, chips)
        pieces.append(lax.dynamic_slice_in_dim(values, k * size, size, axis))
    return jnp.concatenate(pieces, axis=axis)


def near_relative(values, axis):
    half = values.shape[axis] // 2
    other = lax.slice_in_dim(values, half, 2 * half, axis=axis).astype(jnp.bfloat16)
    mine = lax.slice_in_dim(values, 0, half, axis=axis)
    total = mine.astype(jnp.float32) + core_swap(other).astype(jnp.float32)
    return total.astype(jnp.bfloat16)


def far_relative(values, axis):
    chips, _, _ = col_place()
    size = values.shape[axis] // chips
    parts = [lax.slice_in_dim(values, k * size, (k + 1) * size, axis=axis) for k in range(chips)]
    total = parts[0].astype(jnp.float32)
    for s in range(1, chips):
        total = total + col_shift(parts[s], chips - s).astype(jnp.float32)
    return total


def near_natural(values, axis, near):
    chips, _, core = col_place()
    size = values.shape[axis] // (2 * chips)
    split = values.shape[:axis] + (chips, 2, size) + values.shape[axis + 1 :]
    split = values.reshape(split)
    other = lax.dynamic_index_in_dim(split, 1 - core, axis + 1, keepdims=False)
    mine = lax.dynamic_index_in_dim(split, core, axis + 1, keepdims=False)
    return mine.astype(jnp.float32) + core_swap(other.astype(near)).astype(jnp.float32)


def far_natural(values, axis):
    chips, chip, _ = col_place()

    def part(s):
        return lax.dynamic_index_in_dim(values, (chip + s) % chips, axis, keepdims=False)

    total = part(0).astype(jnp.float32)
    for s in range(1, chips):
        total = total + col_shift(part(s).astype(jnp.bfloat16), chips - s).astype(jnp.float32)
    return total


def scatter_natural(values, axis, near):
    return far_natural(near_natural(values, axis, near), axis)


def row_gather(values, axis):
    size = lax.axis_size("row")
    me = lax.axis_index("row")
    shape = list(values.shape)
    shape[axis] = shape[axis] * size
    step = size // 2
    at = axis
    while step:
        got = lax.ppermute(values, "row", [(i, i ^ step) for i in range(size)])
        upper = (me // step) % 2 == 1
        values = jnp.stack(
            [jnp.where(upper, got, values), jnp.where(upper, values, got)], axis=at
        )
        step //= 2
        at += 1
    return values.reshape(shape)


def row_scatter(values):
    size = lax.axis_size("row")
    parts = values.reshape(size, values.shape[0] // size, values.shape[1])
    parts = lax.all_to_all(parts, "row", split_axis=0, concat_axis=0, tiled=True)
    return jnp.sum(parts.astype(jnp.float32), axis=0)


def sum_everywhere(values):
    for name in ("col", "row"):
        size = lax.axis_size(name)
        step = 1
        while step < size:
            values = values + lax.ppermute(values, name, [(i, i ^ step) for i in range(size)])
            step *= 2
    return values


def slot_tables(routes, weights, experts, block):
    first = lax.axis_index("row") * experts
    wanted = (first + jnp.arange(experts, dtype=jnp.int32)).astype(jnp.float32)
    match = routes[:, :, None] == wanted[None, None, :]
    member = jnp.any(match, axis=1)
    weight = jnp.sum(jnp.where(match, weights[:, :, None], 0.0), axis=1)
    blocks = routes.shape[0] // block
    flags = member.astype(jnp.float32).reshape(blocks, block, experts)
    order = jnp.arange(block)
    earlier = (order[None, :] < order[:, None]).astype(jnp.float32)
    inside = jnp.einsum("ij,bje->bie", earlier, flags, preferred_element_type=jnp.float32)
    order = jnp.arange(blocks)
    before = (order[None, :] < order[:, None]).astype(jnp.float32)
    base = jnp.sum(before[:, :, None] * jnp.sum(flags, axis=1)[None], axis=1)
    rank = (inside + base[:, None, :]).reshape(-1, experts).astype(jnp.int32)
    slot = jnp.where(member, rank, -1).T
    slots = jnp.arange(blocks * CAP, dtype=jnp.int32)
    chosen = slot[:, None, :] == slots[None, :, None]
    slot_weight = jnp.sum(jnp.where(chosen, weight.T[:, None, :], 0.0), axis=2)
    return chosen.astype(jnp.bfloat16), slot_weight


def shards(
    block_input,
    segment_ids,
    expert_routes,
    route_weights,
    attn_gain,
    mlp_gain,
    joined_projection_weight,
    output_weight,
    w_gate,
    w_up,
    w_down,
    out_grad,
):
    scaling = HEAD_SIZE ** (-0.5)
    width = joined_projection_weight.shape[1]
    groups = width // (4 * HEAD_SIZE)
    packs_here = segment_ids.shape[0]
    row_count = packs_here * PACKED_LENGTH
    attention_normed, attn_scale = normalize(block_input, attn_gain)
    attention_normed = attention_normed.astype(jnp.bfloat16)
    normed_rows = gather_natural(attention_normed, 0)
    route_rows = row_gather(
        jnp.concatenate([expert_routes.astype(jnp.float32), route_weights], axis=1).T, 1
    ).T
    picks = expert_routes.shape[1]
    experts = w_gate.shape[0]
    chosen, slot_weight = slot_tables(
        route_rows[:, :picks], route_rows[:, picks:], experts, block_input.shape[0]
    )
    pick_matrix = chosen.reshape(-1, chosen.shape[2])
    gate_parts = chip_parts(w_gate)
    up_parts = chip_parts(w_up)
    gate_parts, up_parts, normed_rows, pick_matrix, slot_weight, w_down = lax.optimization_barrier(
        (gate_parts, up_parts, normed_rows, pick_matrix, slot_weight, w_down)
    )
    gate_full = jnp.concatenate(gate_parts + [core_swap(part) for part in gate_parts], axis=1)
    up_full = jnp.concatenate(up_parts + [core_swap(part) for part in up_parts], axis=1)
    down_full = gather_natural(w_down, 1)
    joined = row_gather(jnp.concatenate([joined_projection_weight, output_weight], axis=1), 0)
    late_out_grad, joined = lax.optimization_barrier((out_grad.astype(jnp.bfloat16), joined))
    qkv_full, out_full = joined[:, :width], joined[:, width:]
    cot_rows_in = row_gather(late_out_grad, 0)
    projected = jnp.dot(normed_rows, qkv_full, preferred_element_type=jnp.float32)
    cos_table, sin_forward, swap_matrix = rotary_tables(segment_ids, width)
    prepared = turn_rows(projected, cos_table, sin_forward, swap_matrix).astype(jnp.bfloat16)
    allowed = allowed_table(segment_ids)
    head_outputs = []
    log_totals = []
    for group in range(groups):
        base = group * 4 * HEAD_SIZE
        key_block = head_slice(prepared, base + 2 * HEAD_SIZE, packs_here)
        value_block = head_slice(prepared, base + 3 * HEAD_SIZE, packs_here)
        for inner in range(2):
            query_block = head_slice(prepared, base + inner * HEAD_SIZE, packs_here)
            scored = (
                jnp.einsum(
                    "pqd,pkd->pqk", query_block, key_block, preferred_element_type=jnp.float32
                )
                * scaling
            )
            scored = jnp.where(allowed, scored, -1e30)
            row_max = jnp.max(scored, axis=-1)
            log_total = row_max + jnp.log(jnp.sum(jnp.exp(scored - row_max[..., None]), axis=-1))
            probability = jnp.where(allowed, jnp.exp(scored - log_total[..., None]), 0.0).astype(
                jnp.bfloat16
            )
            result = jnp.einsum(
                "pqk,pkd->pqd", probability, value_block, preferred_element_type=jnp.float32
            ).astype(jnp.bfloat16)
            head_outputs.append(result.reshape(row_count, HEAD_SIZE))
            log_totals.append(log_total)
    heads_flat = jnp.concatenate(head_outputs, axis=1)
    row_block = heads_flat
    attention = scatter_natural(
        jnp.einsum("tj,dj->td", row_block, out_full, preferred_element_type=jnp.float32),
        0,
        jnp.float32,
    )
    residual = block_input + attention
    mlp_normed, mlp_scale = normalize(residual, mlp_gain)
    mlp_normed = mlp_normed.astype(jnp.bfloat16)
    token_rows = row_gather(to_relative(mlp_normed, 1), 0)

    def to_slots(rows):
        return jnp.dot(pick_matrix, rows, preferred_element_type=jnp.float32)

    def to_tokens(rows):
        return lax.dot_general(
            pick_matrix,
            rows.reshape(pick_matrix.shape[0], -1),
            (((0,), (0,)), ((), ())),
            preferred_element_type=jnp.float32,
        ).astype(jnp.bfloat16)

    cot_arrived = (
        (to_slots(cot_rows_in) * slot_weight.reshape(-1, 1))
        .astype(jnp.bfloat16)
        .reshape(experts, -1, cot_rows_in.shape[1])
    )
    act_grad = jnp.einsum(
        "erd,efd->erf", cot_arrived, down_full, preferred_element_type=jnp.float32
    )
    arrived = to_slots(token_rows).astype(jnp.bfloat16).reshape(cot_arrived.shape)
    gate_pre = jnp.einsum("erd,edf->erf", arrived, gate_full, preferred_element_type=jnp.float32)
    up_pre = jnp.einsum("erd,edf->erf", arrived, up_full, preferred_element_type=jnp.float32)
    sigmoid_gate = jax.nn.sigmoid(gate_pre)
    active = (gate_pre * sigmoid_gate * up_pre).astype(jnp.bfloat16)
    gate_grad = (act_grad * up_pre * sigmoid_gate * (1.0 + gate_pre * (1.0 - sigmoid_gate))).astype(
        jnp.bfloat16
    )
    up_grad = (act_grad * gate_pre * sigmoid_gate).astype(jnp.bfloat16)
    row_grad = jnp.einsum("erf,edf->erd", gate_grad, gate_full, preferred_element_type=jnp.float32)
    row_grad = (
        row_grad + jnp.einsum("erf,edf->erd", up_grad, up_full, preferred_element_type=jnp.float32)
    ).astype(jnp.bfloat16)
    mlp_normed_grad = to_natural(row_scatter(to_tokens(row_grad)), 1)
    gate_w_grad = jnp.einsum(
        "erd,erf->edf", arrived, gate_grad, preferred_element_type=jnp.float32
    ).astype(jnp.bfloat16)
    up_w_grad = jnp.einsum(
        "erd,erf->edf", arrived, up_grad, preferred_element_type=jnp.float32
    ).astype(jnp.bfloat16)
    down_grad = jnp.einsum(
        "erf,erd->efd", active, cot_arrived, preferred_element_type=jnp.float32
    ).astype(jnp.bfloat16)
    produced = (
        jnp.einsum("erf,efd->erd", active, down_full, preferred_element_type=jnp.float32)
        * slot_weight[..., None]
    ).astype(jnp.bfloat16)
    produced_rows = to_tokens(produced)
    gate_share = far_relative(near_relative(gate_w_grad, 1), 1)
    up_near = near_relative(up_w_grad, 1)
    down_near = near_natural(down_grad, 1, jnp.bfloat16).astype(jnp.bfloat16)
    mlp_normed_grad, produced_rows, gate_share, up_near, down_near = lax.optimization_barrier(
        (mlp_normed_grad, produced_rows, gate_share, up_near, down_near)
    )
    up_share = far_relative(up_near, 1)
    down_share = far_natural(down_near, 1)
    block_output = residual + row_scatter(produced_rows)
    residual_part, mlp_part = norm_grad(residual, mlp_scale, mlp_gain, mlp_normed_grad)
    residual_grad = out_grad + residual_part
    residual_cotangent = residual_grad.astype(jnp.bfloat16)
    cot_rows = gather_natural(residual_cotangent, 0)
    heads_cotangent = jnp.einsum(
        "td,dj->tj", cot_rows, out_full, preferred_element_type=jnp.float32
    ).astype(jnp.bfloat16)
    out_grad_part = jnp.einsum(
        "td,tj->dj", cot_rows, heads_flat, preferred_element_type=jnp.float32
    )
    grad_pieces = []
    for group in range(groups):
        base = group * 4 * HEAD_SIZE
        key_block = head_slice(prepared, base + 2 * HEAD_SIZE, packs_here)
        value_block = head_slice(prepared, base + 3 * HEAD_SIZE, packs_here)
        key_gradient = jnp.zeros((packs_here, PACKED_LENGTH, HEAD_SIZE), jnp.float32)
        value_gradient = jnp.zeros((packs_here, PACKED_LENGTH, HEAD_SIZE), jnp.float32)
        query_parts = []
        for inner in range(2):
            head_number = 2 * group + inner
            query_block = head_slice(prepared, base + inner * HEAD_SIZE, packs_here)
            cot_block = head_slice(heads_cotangent, head_number * HEAD_SIZE, packs_here)
            result_block = head_slice(heads_flat, head_number * HEAD_SIZE, packs_here)
            scored = (
                jnp.einsum(
                    "pqd,pkd->pqk", query_block, key_block, preferred_element_type=jnp.float32
                )
                * scaling
            )
            scored = jnp.where(allowed, scored, -1e30)
            probability = jnp.where(
                allowed, jnp.exp(scored - log_totals[head_number][..., None]), 0.0
            )
            value_gradient = value_gradient + jnp.einsum(
                "pqk,pqd->pkd",
                probability.astype(jnp.bfloat16),
                cot_block,
                preferred_element_type=jnp.float32,
            )
            prob_grad = jnp.einsum(
                "pqd,pkd->pqk", cot_block, value_block, preferred_element_type=jnp.float32
            )
            row_delta = jnp.einsum(
                "pqd,pqd->pq", cot_block, result_block, preferred_element_type=jnp.float32
            )
            score_grad = (probability * (prob_grad - row_delta[..., None]) * scaling).astype(
                jnp.bfloat16
            )
            query_parts.append(
                jnp.einsum(
                    "pqk,pkd->pqd", score_grad, key_block, preferred_element_type=jnp.float32
                ).reshape(row_count, HEAD_SIZE)
            )
            key_gradient = key_gradient + jnp.einsum(
                "pqk,pqd->pkd", score_grad, query_block, preferred_element_type=jnp.float32
            )
        grad_pieces.extend(query_parts)
        grad_pieces.append(key_gradient.reshape(row_count, HEAD_SIZE))
        grad_pieces.append(value_gradient.reshape(row_count, HEAD_SIZE))
    raw_grad = jnp.concatenate(grad_pieces, axis=1)
    projected_grad = turn_rows(raw_grad, cos_table, -sin_forward, swap_matrix).astype(jnp.bfloat16)
    qkv_grad_part = jnp.einsum(
        "td,tj->dj", normed_rows, projected_grad, preferred_element_type=jnp.float32
    )
    qkv_share = row_scatter(qkv_grad_part.astype(jnp.bfloat16))
    out_share = row_scatter(out_grad_part.astype(jnp.bfloat16))
    row_block = projected_grad
    attn_normed_grad = scatter_natural(
        jnp.einsum("tj,dj->td", row_block, qkv_full, preferred_element_type=jnp.float32),
        0,
        jnp.float32,
    )
    input_part, attn_part = norm_grad(block_input, attn_scale, attn_gain, attn_normed_grad)
    input_grad = residual_grad + input_part
    attn_gain_grad, mlp_gain_grad = sum_everywhere(jnp.stack([attn_part, mlp_part]))
    return (
        block_output,
        input_grad,
        attn_gain_grad,
        mlp_gain_grad,
        qkv_share,
        out_share,
        gate_share,
        up_share,
        down_share,
    )


def solution(mesh):
    in_specs = (
        P(("row", "col"), None),
        P("row", None),
        P(("row", "col"), None),
        P(("row", "col"), None),
        P(),
        P(),
        P("row", "col"),
        P("row", "col"),
        P("row", "col", None),
        P("row", "col", None),
        P("row", "col", None),
        P(("row", "col"), None),
    )
    out_specs = (
        P(("row", "col"), None),
        P(("row", "col"), None),
        P(),
        P(),
        P("row", "col"),
        P("row", "col"),
        P("row", "col", None),
        P("row", "col", None),
        P("row", "col", None),
    )
    return jax.shard_map(shards, mesh=mesh, in_specs=in_specs, out_specs=out_specs, check_vma=False)
```
